32 devices in a mesh: dp: 8 (over y, x, core), tensor: 4 (over z).
Axes of the slice: x: 2, y: 2, z: 4, core: 2. Of those that a mesh axis runs over, the one named last changes fastest.
Arguments:
- block_in: bfloat16 [5832, 1152], P('dp'), may hold values from -40 to 40
- ln1_gain: float32 [1152], replicated, may hold values from 0.5 to 1.5
- ln1_bias: float32 [1152], replicated, may hold values from -4 to 4
- w_qkv: bfloat16 [3, 1152, 1152], P(None, 'dp', 'tensor'), may hold values from -1 to 1
- qv_bias: float32 [2, 1152], P(None, 'tensor'), may hold values from -4 to 4
- w_out: bfloat16 [1152, 1152], P('tensor', 'dp'), may hold values from -3 to 3
- out_bias: float32 [1152], replicated, may hold values from -4 to 4
- ln2_gain: float32 [1152], replicated, may hold values from 0.5 to 1.5
- ln2_bias: float32 [1152], replicated, may hold values from -4 to 4
- w_fc1: bfloat16 [1152, 4304], P('dp', 'tensor'), may hold values from -0.1875 to 0.1875
- fc1_bias: float32 [4304], P('tensor'), may hold values from -4 to 4
- w_fc2: bfloat16 [4304, 1152], P('tensor', 'dp'), may hold values from -0.09375 to 0.09375
- fc2_bias: float32 [1152], replicated, may hold values from -4 to 4
- cotangent: bfloat16 [5832, 1152], P('dp'), may hold values from -50 to 50
Outputs:
- block_out: bfloat16 [5832, 1152], P('dp')
- grad_input: bfloat16 [5832, 1152], P('dp')
- grad_ln1_gain: float32 [1152], replicated
- grad_ln1_bias: float32 [1152], replicated
- grad_w_qkv: float32 [3, 1152, 1152], P(None, 'dp', 'tensor')
- grad_qv_bias: float32 [2, 1152], P(None, 'tensor')
- grad_w_out: float32 [1152, 1152], P('tensor', 'dp')
- grad_out_bias: float32 [1152], replicated
- grad_ln2_gain: float32 [1152], replicated
- grad_ln2_bias: float32 [1152], replicated
- grad_w_fc1: float32 [1152, 4304], P('dp', 'tensor')
- grad_fc1_bias: float32 [4304], P('tensor')
- grad_w_fc2: float32 [4304, 1152], P('tensor', 'dp')
- grad_fc2_bias: float32 [1152], replicated
The draws below stay inside these ranges and needn't reach their ends.
All inputs are finite; a program needn't handle non-finite values.
Results may differ from the reference program's by a relative error of at most 0.02.
Values may be sent and summed in bfloat16 or wider, within the bound.
A program may use at most 128 MiB of HBM per device.

```python
import math
import jax
import jax.numpy as jnp
from jax import lax

HEADS = 16
HEAD_DIM = 72
D = 1152
FF = 4304
SEQ = 729
TOKENS = 5832
N_TENSOR = 4


def draw_block_in(key, part):
    noise_key, row_key, col_key = jax.random.split(jax.random.fold_in(key, 101), 3)
    width = HEADS * HEAD_DIM
    extent = (TOKENS, width)
    noise_part = jax.random.truncated_normal(noise_key, -4.0, 4.0, extent, jnp.float32)
    row_scale = jnp.exp(jax.random.uniform(row_key, (TOKENS, 1), jnp.float32, math.log(0.3), math.log(3.0)))
    col_scale = jnp.exp(jax.random.uniform(col_key, (1, width), jnp.float32, math.log(0.3), math.log(3.0)))
    values = noise_part * row_scale * col_scale
    return values.astype(jnp.bfloat16)


def draw_w_qkv(key, part):
    noise_key = jax.random.fold_in(jax.random.fold_in(key, 202), 0)
    width = HEADS * HEAD_DIM
    spread = width ** (-0.5)
    values = jax.random.truncated_normal(noise_key, -4.0, 4.0, (3, width, width), jnp.float32) * spread
    return values.astype(jnp.bfloat16)


def draw_cotangent(key, part):
    noise_key, row_key, col_key = jax.random.split(jax.random.fold_in(key, 303), 3)
    width = HEADS * HEAD_DIM
    position = jnp.arange(TOKENS, dtype=jnp.float32)[:, None] / max(TOKENS - 1, 1)
    row_jitter = jnp.exp(jax.random.uniform(row_key, (TOKENS, 1), jnp.float32, math.log(0.7), math.log(1.4)))
    col_scale = jnp.exp(jax.random.uniform(col_key, (1, width), jnp.float32, math.log(0.5), math.log(2.0)))
    noise_part = jax.random.truncated_normal(noise_key, -4.0, 4.0, (TOKENS, width), jnp.float32)
    rising = jnp.exp(math.log(3.0) * position)
    values = noise_part * rising * row_jitter * col_scale
    return values.astype(jnp.bfloat16)


def shard_levels(stream_key, shape, pieces, low, top_value):
    loudness, own = 1.0, jax.random.fold_in(stream_key, 6)
    for dim, blocks in pieces:
        draws = jnp.exp(jax.random.uniform(jax.random.fold_in(own, dim), (blocks,), jnp.float32, low / len(pieces), top_value / len(pieces)))
        loudness = loudness * jnp.repeat(draws, shape[dim] // blocks).reshape([-1 if axis == dim else 1 for axis in range(len(shape))])
    return loudness


def centred(stream_key, shape, scale, reach, shards=(), kind=jnp.bfloat16):
    values = jax.random.normal(stream_key, shape, jnp.float32) * scale
    if len(shards) > 0:
        values = shard_levels(stream_key, shape, shards, -0.22, 0.18) * values
    return jnp.clip(values, min=-reach, max=reach).astype(kind)


def setup_inputs(seed: int = 0) -> dict:
    seeds = jax.random.split(jax.random.key(seed), 15)
    return {
        "block_in": draw_block_in(jax.random.fold_in(seeds[14], 71), 0),
        "ln1_gain": jnp.clip(1.0 + 0.1 * jax.random.normal(seeds[1], (D,), jnp.float32), 0.5, 1.5),
        "ln1_bias": centred(seeds[2], (D,), 0.3, 4.0, (), jnp.float32),
        "w_qkv": draw_w_qkv(jax.random.fold_in(seeds[14], 71), 0),
        "qv_bias": centred(seeds[4], (2, D), 0.5, 4.0, ((1, 4),), jnp.float32),
        "w_out": centred(seeds[5], (D, D), (max(1, D // 256)) ** -0.5, 3.0, ((0, 4), (1, 8))),
        "out_bias": centred(seeds[6], (D,), 0.3, 4.0, (), jnp.float32),
        "ln2_gain": jnp.clip(1.0 + 0.1 * jax.random.normal(seeds[7], (D,), jnp.float32), 0.5, 1.5),
        "ln2_bias": centred(seeds[8], (D,), 0.3, 4.0, (), jnp.float32),
        "w_fc1": centred(seeds[9], (D, FF), D ** -0.5, 0.1875, ((0, 8), (1, 4))),
        "fc1_bias": centred(seeds[10], (FF,), 0.5, 4.0, ((0, 4),), jnp.float32),
        "w_fc2": centred(seeds[11], (FF, D), FF ** -0.5, 0.09375, ((0, 4), (1, 8))),
        "fc2_bias": centred(seeds[12], (D,), 0.3, 4.0, (), jnp.float32),
        "cotangent": draw_cotangent(jax.random.fold_in(seeds[14], 71), 0),
    }


GELU_C = 0.7978845608028654
CUBIC_C = 0.044715
LN_EPS = 1e-06

def norm_forward(values, norm_gain, norm_shift):
    center = lax.optimization_barrier(jnp.mean(values, axis=-1, keepdims=True))
    offset = values - center
    spread = lax.optimization_barrier(jnp.mean(offset * offset, axis=-1, keepdims=True))
    inv_std = lax.rsqrt(spread + LN_EPS)
    scaled = offset * inv_std
    return (scaled * norm_gain + norm_shift, scaled, inv_std)

def norm_backward(upstream, norm_gain, scaled, inv_std):
    weighted = upstream * norm_gain
    inner_term = weighted - lax.optimization_barrier(jnp.mean(weighted, axis=-1, keepdims=True)) - scaled * lax.optimization_barrier(jnp.mean(weighted * scaled, axis=-1, keepdims=True))
    return (inv_std * inner_term, lax.optimization_barrier(jnp.sum(upstream * scaled, axis=0)), lax.optimization_barrier(jnp.sum(upstream, axis=0)))

def gelu_value(pre_act):
    square = pre_act * pre_act
    tangent = jnp.tanh(GELU_C * (pre_act + CUBIC_C * square * pre_act))
    return 0.5 * pre_act * (1.0 + tangent)

def gelu_slope(pre_act):
    square = pre_act * pre_act
    tangent = jnp.tanh(GELU_C * (pre_act + CUBIC_C * square * pre_act))
    return 0.5 * (1.0 + tangent) + 0.5 * pre_act * (1.0 - tangent * tangent) * GELU_C * (1.0 + 3.0 * CUBIC_C * square)

def tensor_sum(partials):
    lowered = lax.optimization_barrier(partials.astype(jnp.bfloat16))
    return lax.optimization_barrier(jnp.sum(lowered.astype(jnp.float32), axis=0))

def attend(queries, keys_in, values_in):
    score_scale = queries.shape[2] ** (-0.5)
    scores = jnp.einsum('qhd,khd->hqk', queries.astype(jnp.float32), keys_in.astype(jnp.float32)) * score_scale
    row_max = lax.optimization_barrier(jnp.max(scores, axis=2, keepdims=True))
    lifted = jnp.exp(scores - row_max)
    row_total = lax.optimization_barrier(jnp.sum(lifted, axis=2, keepdims=True))
    attn_probs = (lifted / row_total).astype(jnp.bfloat16)
    mixed_out = jnp.einsum('hqk,khd->qhd', attn_probs.astype(jnp.float32), values_in.astype(jnp.float32))
    return (mixed_out.astype(jnp.bfloat16), row_max + jnp.log(row_total))

def attend_back(queries, keys_in, values_in, mixed_out, log_total, grad_mixed):
    score_scale = queries.shape[2] ** (-0.5)
    scores = jnp.einsum('qhd,khd->hqk', queries.astype(jnp.float32), keys_in.astype(jnp.float32)) * score_scale
    probs_back = jnp.exp(scores - log_total)
    probs_low = probs_back.astype(jnp.bfloat16)
    grad_values = jnp.einsum('hqk,qhd->khd', probs_low.astype(jnp.float32), grad_mixed.astype(jnp.float32))
    grad_probs = jnp.einsum('qhd,khd->hqk', grad_mixed.astype(jnp.float32), values_in.astype(jnp.float32))
    carried = lax.optimization_barrier(jnp.sum(grad_mixed.astype(jnp.float32) * mixed_out.astype(jnp.float32), axis=2))
    carried = jnp.transpose(carried)[:, :, None]
    grad_scores = (probs_back * (grad_probs - carried) * score_scale).astype(jnp.bfloat16)
    grad_queries = jnp.einsum('hqk,khd->qhd', grad_scores.astype(jnp.float32), keys_in.astype(jnp.float32))
    grad_keys = jnp.einsum('hqk,qhd->khd', grad_scores.astype(jnp.float32), queries.astype(jnp.float32))
    return (grad_queries, grad_keys, grad_values)

def one_image(weights, rows_low, grad_low):
    ln1_gain, ln1_bias, w_qkv, qv_bias, w_out, out_bias, ln2_gain, ln2_bias, w_fc1, fc1_bias, w_fc2, fc2_bias = weights
    groups = N_TENSOR
    per_group = D // groups
    units = FF // groups
    rows_in = rows_low.astype(jnp.float32)
    normed_one, scaled_one, inv_one = norm_forward(rows_in, ln1_gain, ln1_bias)
    normed_low = normed_one.astype(jnp.bfloat16)
    bias_rows = jnp.stack([qv_bias[0], jnp.zeros_like(qv_bias[0]), qv_bias[1]])
    project = jnp.einsum('sd,cdk->csk', normed_low.astype(jnp.float32), w_qkv.astype(jnp.float32)) + bias_rows[:, None, :]
    project_low = project.astype(jnp.bfloat16)
    heads_view = project_low.reshape(3, SEQ, HEADS, HEAD_DIM)
    mixed_out, log_total = attend(heads_view[0], heads_view[1], heads_view[2])
    mixed_flat = mixed_out.reshape(SEQ, D)
    attn_parts = jnp.einsum('sgk,gkd->gsd', mixed_flat.reshape(SEQ, groups, per_group).astype(jnp.float32), w_out.reshape(groups, per_group, D).astype(jnp.float32))
    middle = rows_in + tensor_sum(attn_parts) + out_bias
    normed_two, scaled_two, inv_two = norm_forward(middle, ln2_gain, ln2_bias)
    normed_low2 = normed_two.astype(jnp.bfloat16)
    pre_act = jnp.dot(normed_low2, w_fc1, preferred_element_type=jnp.float32) + fc1_bias
    act_low = gelu_value(pre_act).astype(jnp.bfloat16)
    mlp_parts = jnp.einsum('sgf,gfd->gsd', act_low.reshape(SEQ, groups, units).astype(jnp.float32), w_fc2.reshape(groups, units, D).astype(jnp.float32))
    result = (middle + tensor_sum(mlp_parts) + fc2_bias).astype(jnp.bfloat16)
    upstream = grad_low.astype(jnp.float32)
    grad_fc2_bias = lax.optimization_barrier(jnp.sum(upstream, axis=0))
    grad_w_fc2 = jnp.dot(act_low.T, grad_low, preferred_element_type=jnp.float32)
    grad_act = jnp.dot(grad_low, w_fc2.T, preferred_element_type=jnp.float32)
    grad_pre = grad_act * gelu_slope(pre_act)
    grad_fc1_bias = lax.optimization_barrier(jnp.sum(grad_pre, axis=0))
    grad_pre_low = grad_pre.astype(jnp.bfloat16)
    grad_w_fc1 = jnp.dot(normed_low2.T, grad_pre_low, preferred_element_type=jnp.float32)
    back_parts = jnp.einsum('sgf,dgf->gsd', grad_pre_low.reshape(SEQ, groups, units).astype(jnp.float32), w_fc1.reshape(D, groups, units).astype(jnp.float32))
    back_two = tensor_sum(back_parts)
    grad_norm2, grad_ln2_gain, grad_ln2_bias = norm_backward(back_two, ln2_gain, scaled_two, inv_two)
    grad_middle = upstream + grad_norm2
    grad_out_bias = lax.optimization_barrier(jnp.sum(grad_middle, axis=0))
    grad_middle_low = grad_middle.astype(jnp.bfloat16)
    grad_w_out = jnp.dot(mixed_flat.T, grad_middle_low, preferred_element_type=jnp.float32)
    grad_mixed = jnp.dot(grad_middle_low, w_out.T, preferred_element_type=jnp.float32).astype(jnp.bfloat16)
    grad_mixed = grad_mixed.reshape(SEQ, HEADS, HEAD_DIM)
    grad_queries, grad_keys, grad_values = attend_back(heads_view[0], heads_view[1], heads_view[2], mixed_out, log_total, grad_mixed)
    grad_queries = grad_queries.reshape(SEQ, D)
    grad_keys = grad_keys.reshape(SEQ, D)
    grad_values = grad_values.reshape(SEQ, D)
    grad_qv_bias = jnp.stack([lax.optimization_barrier(jnp.sum(grad_queries, axis=0)), lax.optimization_barrier(jnp.sum(grad_values, axis=0))])
    grad_proj = jnp.stack([grad_queries, grad_keys, grad_values]).astype(jnp.bfloat16)
    grad_w_qkv = jnp.einsum('sd,csk->cdk', normed_low.astype(jnp.float32), grad_proj.astype(jnp.float32))
    first_parts = jnp.einsum('csgk,cdgk->gsd', grad_proj.reshape(3, SEQ, groups, per_group).astype(jnp.float32), w_qkv.reshape(3, D, groups, per_group).astype(jnp.float32))
    back_one = tensor_sum(first_parts)
    grad_norm1, grad_ln1_gain, grad_ln1_bias = norm_backward(back_one, ln1_gain, scaled_one, inv_one)
    grad_rows = (grad_middle + grad_norm1).astype(jnp.bfloat16)
    grads = (grad_ln1_gain, grad_ln1_bias, grad_w_qkv, grad_qv_bias, grad_w_out, grad_out_bias, grad_ln2_gain, grad_ln2_bias, grad_w_fc1, grad_fc1_bias, grad_w_fc2, grad_fc2_bias)
    return (result, grad_rows, grads)

def reference(block_in, ln1_gain, ln1_bias, w_qkv, qv_bias, w_out, out_bias, ln2_gain, ln2_bias, w_fc1, fc1_bias, w_fc2, fc2_bias, cotangent):
    images = TOKENS // SEQ
    weights = (ln1_gain, ln1_bias, w_qkv, qv_bias, w_out, out_bias, ln2_gain, ln2_bias, w_fc1, fc1_bias, w_fc2, fc2_bias)
    initial = tuple((jnp.zeros(member.shape, jnp.float32) for member in weights))

    def advance(carry, paired):
        rows_low, grad_low = paired
        result, grad_rows, grads = one_image(weights, rows_low, grad_low)
        return (jax.tree.map(jnp.add, carry, grads), (result, grad_rows))
    totals, stacked = lax.scan(advance, initial, (block_in.reshape(images, SEQ, D), cotangent.reshape(images, SEQ, D)))
    block_out = stacked[0].reshape(TOKENS, D)
    grad_input = stacked[1].reshape(TOKENS, D)
    g_one, b_one, g_qkv, g_qv, g_out, g_outb, g_two, b_two, g_fc1, g_fc1b, g_fc2, g_fc2b = totals
    return (block_out, grad_input, g_one, b_one, g_qkv, g_qv, g_out, g_outb, g_two, b_two, g_fc1, g_fc1b, g_fc2, g_fc2b)
```

```python
import functools

import jax
import jax.numpy as jnp
from jax import lax
from jax.experimental import pallas as pl
from jax.experimental.pallas import tpu as pltpu
from jax.sharding import PartitionSpec as P

HEAD_DIM = 72
SEQ = 729


GELU_C = 0.7978845608028654
CUBIC_C = 0.044715
LN_EPS = 1e-06


def norm_forward(values, norm_gain, norm_shift):
    center = jnp.mean(values, axis=-1, keepdims=True)
    offset = values - center
    spread = jnp.mean(offset * offset, axis=-1, keepdims=True)
    inv_std = lax.rsqrt(spread + LN_EPS)
    scaled = offset * inv_std
    return (scaled * norm_gain + norm_shift, scaled, inv_std)


def norm_backward(upstream, norm_gain, scaled, inv_std):
    weighted = upstream * norm_gain
    inner_term = (
        weighted
        - jnp.mean(weighted, axis=-1, keepdims=True)
        - scaled * jnp.mean(weighted * scaled, axis=-1, keepdims=True)
    )
    return (inv_std * inner_term, jnp.sum(upstream * scaled, axis=0), jnp.sum(upstream, axis=0))


def gelu_value(pre_act):
    square = pre_act * pre_act
    tangent = jnp.tanh(GELU_C * (pre_act + CUBIC_C * square * pre_act))
    return 0.5 * pre_act * (1.0 + tangent)


def gelu_slope(pre_act):
    square = pre_act * pre_act
    tangent = jnp.tanh(GELU_C * (pre_act + CUBIC_C * square * pre_act))
    return 0.5 * (1.0 + tangent) + 0.5 * pre_act * (1.0 - tangent * tangent) * GELU_C * (
        1.0 + 3.0 * CUBIC_C * square
    )


def attend(queries, keys_in, values_in):
    score_scale = queries.shape[2] ** (-0.5)
    scores = (
        jnp.einsum("qhd,khd->hqk", queries, keys_in, preferred_element_type=jnp.float32)
        * score_scale
    )
    row_max = jnp.max(scores, axis=2, keepdims=True)
    lifted = jnp.exp(scores - row_max)
    row_total = jnp.sum(lifted, axis=2, keepdims=True)
    attn_probs = (lifted / row_total).astype(jnp.bfloat16)
    mixed_out = jnp.einsum(
        "hqk,khd->qhd", attn_probs, values_in, preferred_element_type=jnp.float32
    )
    return (mixed_out.astype(jnp.bfloat16), row_max + jnp.log(row_total))


def attend_back(queries, keys_in, values_in, mixed_out, log_total, grad_mixed):
    score_scale = queries.shape[2] ** (-0.5)
    scores = (
        jnp.einsum("qhd,khd->hqk", queries, keys_in, preferred_element_type=jnp.float32)
        * score_scale
    )
    probs_back = jnp.exp(scores - log_total)
    probs_low = probs_back.astype(jnp.bfloat16)
    grad_values = jnp.einsum(
        "hqk,qhd->khd", probs_low, grad_mixed, preferred_element_type=jnp.float32
    )
    grad_probs = jnp.einsum(
        "qhd,khd->hqk", grad_mixed, values_in, preferred_element_type=jnp.float32
    )
    carried = jnp.sum(grad_mixed.astype(jnp.float32) * mixed_out.astype(jnp.float32), axis=2)
    carried = jnp.transpose(carried)[:, :, None]
    grad_scores = (probs_back * (grad_probs - carried) * score_scale).astype(jnp.bfloat16)
    grad_queries = jnp.einsum(
        "hqk,khd->qhd", grad_scores, keys_in, preferred_element_type=jnp.float32
    )
    grad_keys = jnp.einsum("hqk,qhd->khd", grad_scores, queries, preferred_element_type=jnp.float32)
    return (grad_queries, grad_keys, grad_values)


LANES = 128


def line_sum_kernel(size, count, *refs):
    parts, results = refs[:count], refs[count : 2 * count]
    inward, summed, inner_in, in_send, in_recv, out_send, out_recv = refs[2 * count :]
    columns = parts[0].shape[1] // LANES
    chunks = count * columns
    me = lax.axis_index("tensor")
    half = size // 2
    low = me < half
    inner = jnp.where(low, me + 1, me - 1)
    outer = jnp.where(low, me - 1, me + 1)
    at_end = (me == 0) | (me == size - 1)
    at_mid = (me == half - 1) | (me == half)
    inner = jnp.clip(inner, 0, size - 1)
    outer = jnp.clip(outer, 0, size - 1)

    barrier = pltpu.get_barrier_semaphore()
    pl.semaphore_signal(
        barrier, inc=1, device_id={"tensor": inner}, device_id_type=pl.DeviceIdType.MESH
    )

    @pl.when(jnp.logical_not(at_end))
    def _():
        pl.semaphore_signal(
            barrier, inc=1, device_id={"tensor": outer}, device_id_type=pl.DeviceIdType.MESH
        )

    pl.semaphore_wait(barrier, jnp.where(at_end, 1, 2))

    def own(c):
        return parts[c // columns].at[:, pl.ds((c % columns) * LANES, LANES)]

    def result(c):
        return results[c // columns].at[:, pl.ds((c % columns) * LANES, LANES)]

    def send_in(c, source, landing):
        return pltpu.make_async_remote_copy(
            src_ref=source,
            dst_ref=landing.at[c],
            send_sem=in_send.at[c],
            recv_sem=(out_recv if landing is inner_in else in_recv).at[c],
            device_id={"tensor": inner},
            device_id_type=pl.DeviceIdType.MESH,
        )

    def send_out(c, source):
        return pltpu.make_async_remote_copy(
            src_ref=source,
            dst_ref=inner_in.at[c],
            send_sem=out_send.at[c],
            recv_sem=out_recv.at[c],
            device_id={"tensor": outer},
            device_id_type=pl.DeviceIdType.MESH,
        )

    def add_outer(c):
        send_in(c, own(c), inward).wait_recv()
        summed[c] = (
            own(c)[...].astype(jnp.float32) + inward[c].astype(jnp.float32)
        ).astype(jnp.bfloat16)

    def wait_inner(c):
        send_out(c, inner_in.at[c]).wait_recv()

    if size > 2:

        @pl.when(at_end)
        def _():
            for c in range(chunks):
                send_in(c, own(c), inward).start()
            for c in range(chunks):
                wait_inner(c)
                result(c)[...] = inner_in[c]
            for c in range(chunks):
                send_in(c, own(c), inward).wait_send()

    if size > 4:

        @pl.when(jnp.logical_not(at_end | at_mid))
        def _():
            for c in range(chunks):
                add_outer(c)
                send_in(c, summed.at[c], inward).start()
            for c in range(chunks):
                wait_inner(c)
                send_out(c, inner_in.at[c]).start()
                result(c)[...] = inner_in[c]
            for c in range(chunks):
                send_in(c, summed.at[c], inward).wait_send()
                send_out(c, inner_in.at[c]).wait_send()

    @pl.when(at_mid)
    def _():
        def finish(c):
            wait_inner(c)
            result(c)[...] = (
                summed[c].astype(jnp.float32) + inner_in[c].astype(jnp.float32)
            ).astype(jnp.bfloat16)
            if size > 2:
                send_out(c, result(c)).start()

        for c in range(chunks):
            if size > 2:
                add_outer(c)
            else:
                summed[c] = own(c)[...]
            send_in(c, summed.at[c], inner_in).start()
            if c > 0:
                finish(c - 1)
        finish(chunks - 1)
        for c in range(chunks):
            send_in(c, summed.at[c], inner_in).wait_send()
            if size > 2:
                send_out(c, result(c)).wait_send()


def line_sum(parts, size, call_id):
    rows, width = parts[0].shape
    count = len(parts)
    chunks = count * (width // LANES)
    slots = pltpu.VMEM((chunks, rows, LANES), jnp.bfloat16)
    semaphores = pltpu.SemaphoreType.DMA((chunks,))
    total_bytes = count * rows * width * 2
    return pl.pallas_call(
        functools.partial(line_sum_kernel, size, count),
        out_shape=[jax.ShapeDtypeStruct((rows, width), jnp.bfloat16)] * count,
        in_specs=[pl.BlockSpec(memory_space=pltpu.VMEM)] * count,
        out_specs=[pl.BlockSpec(memory_space=pltpu.VMEM)] * count,
        scratch_shapes=[slots, slots, slots, semaphores, semaphores, semaphores, semaphores],
        compiler_params=pltpu.CompilerParams(
            collective_id=call_id, has_side_effects=True, vmem_limit_bytes=40 * 2**20
        ),
        cost_estimate=pl.CostEstimate(
            flops=0, bytes_accessed=100 * total_bytes, transcendentals=0
        ),
        name=f"line_sum_{call_id}",
    )(*parts)


def image_sum_kernel(size, part_ref, total_ref, slots, send_sem, recv_sem):
    me = lax.axis_index("dp")
    barrier = pltpu.get_barrier_semaphore()
    for step in range(1, size):
        pl.semaphore_signal(
            barrier,
            inc=1,
            device_id={"dp": lax.rem(me + step, size)},
            device_id_type=pl.DeviceIdType.MESH,
        )
    pl.semaphore_wait(barrier, size - 1)

    def send(step, slot):
        return pltpu.make_async_remote_copy(
            src_ref=part_ref,
            dst_ref=slots.at[slot],
            send_sem=send_sem.at[step],
            recv_sem=recv_sem.at[step],
            device_id={"dp": lax.rem(me + step, size)},
            device_id_type=pl.DeviceIdType.MESH,
        )

    for step in range(1, size):
        send(step, me).start()
    slots[me] = part_ref[...]
    for step in range(1, size):
        send(step, lax.rem(me + size - step, size)).wait_recv()
    total = slots[0]
    for member in range(1, size):
        total = total + slots[member]
    total_ref[...] = total
    for step in range(1, size):
        send(step, me).wait_send()


def image_sum(arrays, size, call_id):
    flat = jnp.concatenate([array.reshape(-1) for array in arrays])
    tile = 8 * LANES
    padded = -(-flat.shape[0] // tile) * tile
    packed = jnp.pad(flat, (0, padded - flat.shape[0])).reshape(-1, LANES)
    total = pl.pallas_call(
        functools.partial(image_sum_kernel, size),
        out_shape=jax.ShapeDtypeStruct(packed.shape, jnp.float32),
        in_specs=[pl.BlockSpec(memory_space=pltpu.VMEM)],
        out_specs=pl.BlockSpec(memory_space=pltpu.VMEM),
        scratch_shapes=[
            pltpu.VMEM((size,) + packed.shape, jnp.float32),
            pltpu.SemaphoreType.DMA((size,)),
            pltpu.SemaphoreType.DMA((size,)),
        ],
        compiler_params=pltpu.CompilerParams(collective_id=call_id, has_side_effects=True),
        name="image_sum",
    )(packed).reshape(-1)
    sums, start = [], 0
    for array in arrays:
        sums.append(total[start : start + array.size].reshape(array.shape))
        start += array.size
    return sums


def fetch_forward(w_qkv, w_out, w_fc1, w_fc2):
    return (
        lax.all_gather(w_qkv, "dp", axis=1, tiled=True),
        lax.all_gather(w_out, "dp", axis=1, tiled=True),
        lax.all_gather(w_fc1, "dp", axis=0, tiled=True),
        lax.all_gather(w_fc2, "dp", axis=1, tiled=True),
    )


def shards(
    images,
    groups,
    block_in,
    ln1_gain,
    ln1_bias,
    w_qkv,
    qv_bias,
    w_out,
    out_bias,
    ln2_gain,
    ln2_bias,
    w_fc1,
    fc1_bias,
    w_fc2,
    fc2_bias,
    cotangent,
):
    local_width = w_qkv.shape[2]
    head_count = local_width // HEAD_DIM
    bias_rows = jnp.stack([qv_bias[0], jnp.zeros_like(qv_bias[0]), qv_bias[1]])
    weights = fetch_forward(w_qkv, w_out, w_fc1, w_fc2)
    full_qkv, full_out, full_fc1, full_fc2 = weights
    rows_in = block_in.astype(jnp.float32)
    normed_one, scaled_one, inv_one = norm_forward(rows_in, ln1_gain, ln1_bias)
    normed_low = normed_one.astype(jnp.bfloat16)
    project = (
        jnp.einsum("sd,cdk->csk", normed_low, full_qkv, preferred_element_type=jnp.float32)
        + bias_rows[:, None, :]
    )
    project_low = project.astype(jnp.bfloat16)
    heads_view = project_low.reshape(3, SEQ, head_count, HEAD_DIM)
    mixed_out, log_total = attend(heads_view[0], heads_view[1], heads_view[2])
    mixed_flat = mixed_out.reshape(SEQ, local_width)
    attn_part = jnp.dot(mixed_flat, full_out, preferred_element_type=jnp.float32)
    (attn_whole,) = line_sum([attn_part.astype(jnp.bfloat16)], groups, 0)
    attn_whole = attn_whole.astype(jnp.float32)
    middle = rows_in + attn_whole + out_bias
    normed_two, scaled_two, inv_two = norm_forward(middle, ln2_gain, ln2_bias)
    normed_low2 = normed_two.astype(jnp.bfloat16)
    pre_act = jnp.dot(normed_low2, full_fc1, preferred_element_type=jnp.float32) + fc1_bias
    act_low = gelu_value(pre_act).astype(jnp.bfloat16)
    mlp_part = jnp.dot(act_low, full_fc2, preferred_element_type=jnp.float32)
    upstream = cotangent.astype(jnp.float32)
    acc_fc2 = jnp.einsum("sd,sf->df", cotangent, act_low, preferred_element_type=jnp.float32)
    grad_act = jnp.einsum("sd,fd->sf", cotangent, full_fc2, preferred_element_type=jnp.float32)
    grad_pre = grad_act * gelu_slope(pre_act)
    grad_pre_low = grad_pre.astype(jnp.bfloat16)
    acc_fc1 = jnp.einsum("sd,sf->df", normed_low2, grad_pre_low, preferred_element_type=jnp.float32)
    back_part = jnp.einsum("sf,df->sd", grad_pre_low, full_fc1, preferred_element_type=jnp.float32)
    back_part = back_part.astype(jnp.bfloat16)
    shard_fc2 = lax.psum_scatter(acc_fc2.astype(jnp.bfloat16), "dp", scatter_dimension=0, tiled=True)
    shard_fc1 = lax.psum_scatter(acc_fc1.astype(jnp.bfloat16), "dp", scatter_dimension=0, tiled=True)
    (back_two,) = line_sum([back_part], groups, 1)
    back_two = back_two.astype(jnp.float32)
    grad_norm2, gain_two, shift_two = norm_backward(back_two, ln2_gain, scaled_two, inv_two)
    grad_middle = upstream + grad_norm2
    grad_middle_low = grad_middle.astype(jnp.bfloat16)
    acc_out = jnp.einsum(
        "sd,sk->dk", grad_middle_low, mixed_flat, preferred_element_type=jnp.float32
    )
    grad_mixed = jnp.einsum(
        "sd,kd->sk", grad_middle_low, full_out, preferred_element_type=jnp.float32
    ).astype(jnp.bfloat16)
    grad_mixed = grad_mixed.reshape(SEQ, head_count, HEAD_DIM)
    grad_queries, grad_keys, grad_values = attend_back(
        heads_view[0], heads_view[1], heads_view[2], mixed_out, log_total, grad_mixed
    )
    grad_queries = grad_queries.reshape(SEQ, local_width)
    grad_keys = grad_keys.reshape(SEQ, local_width)
    grad_values = grad_values.reshape(SEQ, local_width)
    grad_proj = jnp.stack([grad_queries, grad_keys, grad_values]).astype(jnp.bfloat16)
    flat_proj = jnp.concatenate([grad_proj[0], grad_proj[1], grad_proj[2]], axis=1)
    acc_qkv = jnp.einsum("sd,sk->dk", normed_low, flat_proj, preferred_element_type=jnp.float32)
    first_part = jnp.einsum("csk,cdk->sd", grad_proj, full_qkv, preferred_element_type=jnp.float32)
    acc_out, acc_qkv, shard_fc1, shard_fc2 = lax.optimization_barrier(
        (acc_out.astype(jnp.bfloat16), acc_qkv.astype(jnp.bfloat16), shard_fc1, shard_fc2)
    )
    shard_out = lax.psum_scatter(acc_out, "dp", scatter_dimension=0, tiled=True)
    shard_qkv = lax.psum_scatter(acc_qkv, "dp", scatter_dimension=0, tiled=True)
    back_one, mlp_whole = line_sum(
        [first_part.astype(jnp.bfloat16), mlp_part.astype(jnp.bfloat16)], groups, 2
    )
    back_one = back_one.astype(jnp.float32)
    results_out = (middle + mlp_whole.astype(jnp.float32) + fc2_bias).astype(jnp.bfloat16)
    grad_norm1, gain_one, shift_one = norm_backward(back_one, ln1_gain, scaled_one, inv_one)
    results_grad = (grad_middle + grad_norm1).astype(jnp.bfloat16)
    image_rows = (gain_one, shift_one, jnp.sum(grad_middle, axis=0), gain_two, shift_two)
    image_units = (
        jnp.stack([jnp.sum(grad_queries, axis=0), jnp.sum(grad_values, axis=0)]),
        jnp.sum(grad_pre, axis=0),
        jnp.sum(upstream, axis=0),
    )
    shard_qkv = shard_qkv.astype(jnp.float32).reshape(-1, 3, local_width).transpose(1, 0, 2)
    shard_out = shard_out.astype(jnp.float32).transpose()
    shard_fc1 = shard_fc1.astype(jnp.float32)
    shard_fc2 = shard_fc2.astype(jnp.float32).transpose()
    sum_g1, sum_b1, sum_ob, sum_g2, sum_b2, sum_qv, sum_f1, sum_f2 = image_sum(
        image_rows + image_units, images, 3
    )
    return (
        results_out,
        results_grad,
        sum_g1,
        sum_b1,
        shard_qkv,
        sum_qv,
        shard_out,
        sum_ob,
        sum_g2,
        sum_b2,
        shard_fc1,
        sum_f1,
        shard_fc2,
        sum_f2,
    )


def solution(mesh):
    placed = (
        P("dp", None),
        P(),
        P(),
        P(None, "dp", "tensor"),
        P(None, "tensor"),
        P("tensor", "dp"),
        P(),
        P(),
        P(),
        P("dp", "tensor"),
        P("tensor"),
        P("tensor", "dp"),
        P(),
        P("dp", None),
    )
    return jax.shard_map(
        functools.partial(shards, mesh.shape["dp"], mesh.shape["tensor"]),
        mesh=mesh,
        in_specs=placed,
        out_specs=(
            P("dp", None),
            P("dp", None),
            P(),
            P(),
            P(None, "dp", "tensor"),
            P(None, "tensor"),
            P("tensor", "dp"),
            P(),
            P(),
            P(),
            P("dp", "tensor"),
            P("tensor"),
            P("tensor", "dp"),
            P(),
        ),
        check_vma=False,
    )
```
